32 devices in a mesh: sec: 8 (over y, x, core), ch: 4 (over z).
Axes of the slice: x: 2, y: 2, z: 4, core: 2. Of those that a mesh axis runs over, the one named last changes fastest.
Arguments:
- start_amps: bfloat16 [6, 1024, 2048], P(None, 'ch'), may hold values from -6 to 6
- energies: float32 [6], replicated, may hold values from 0.5 to 2
- thresholds: bfloat16 [8, 1024], P('sec', 'ch'), may hold values from -3 to -1
- intersection: bfloat16 [8, 1024, 1024], P('sec', 'ch'), may hold values from -0.2 to 1
Outputs:
- boundary_amps: bfloat16 [8, 6, 1024, 2048], P('sec', None, 'ch')
The draws below stay inside these ranges and needn't reach their ends.
All inputs are finite; a program needn't handle non-finite values.
Results may differ from the reference program's by a relative error of at most 0.04.
Values may be sent and summed in bfloat16 or wider, within the bound.
A program may use at most 64 MiB of HBM per device.

```python
import math
import jax
import jax.numpy as jnp
from jax import lax

CH = 1024
NV = 1024
NE = 6
SECTORS = 8


def draw_intersection(key, part):
    spread = jax.random.truncated_normal(key, -4.0, 4.0, (SECTORS, CH, CH), jnp.float32) * (0.25 / math.sqrt(2.0 * CH))
    skewed = spread - jnp.swapaxes(spread, 1, 2)
    identity = jnp.eye(CH, dtype=jnp.float32)[None, :, :]
    return ((identity + skewed) / math.sqrt(1.0625)).astype(jnp.bfloat16)


def steps_of(key, extent, shards, low, largest):
    def one(axis_at, parts):
        draws = jax.random.uniform(jax.random.fold_in(jax.random.fold_in(key, 6), axis_at), (parts,), jnp.float32, low / len(shards), largest / len(shards))
        return jnp.repeat(jnp.exp(draws), extent[axis_at] // parts).reshape((-1,) + (1,) * (len(extent) - axis_at - 1))

    loudness = one(*shards[0])
    for cut in shards[1:]:
        loudness = loudness * one(*cut)
    return loudness


def scatter_about(rng, shape, scale, limit, cuts=(), kind=jnp.bfloat16):
    array = scale * jax.random.normal(rng, shape, jnp.float32)
    if cuts:
        array = array * steps_of(rng, shape, cuts, -0.22, 0.18)
    return jnp.clip(array, -limit, limit).astype(kind)


def setup_inputs(seed: int = 0) -> dict:
    keys = jax.random.split(jax.random.key(seed), 5)
    return {
        "start_amps": scatter_about(keys[0], (NE, CH, 2 * NV), 1.0, 6.0, ((1, 4),)),
        "energies": jnp.clip(jax.random.uniform(keys[1], (NE,), jnp.float32, 0.5, 2.0), 0.5, 2.0),
        "thresholds": jnp.clip(-3.0 + 2.0 * jax.random.uniform(keys[2], (SECTORS, CH), jnp.float32) ** steps_of(keys[2], (SECTORS, CH), ((0, 8), (1, 4)), -0.2, 0.2), -3.0, -1.0).astype(jnp.bfloat16),
        "intersection": draw_intersection(jax.random.fold_in(keys[4], 71), 0),
    }


def rotate(amplitude, wavenumber):
    half = amplitude.shape[-1] // 2
    values_part = amplitude[..., :half]
    slopes_part = amplitude[..., half:]
    cosine = jnp.cos(wavenumber)
    sine_term = jnp.sin(wavenumber)
    new_values = cosine * values_part + sine_term / wavenumber * slopes_part
    new_slopes = -wavenumber * sine_term * values_part + cosine * slopes_part
    return jnp.concatenate([new_values, new_slopes], axis=-1)

def reference(start_amps, energies, thresholds, intersection):

    def advance(amplitude, sector_data):
        channel_thresholds, basis_change = sector_data
        wavenumber = jnp.sqrt(energies[:, None] - channel_thresholds.astype(jnp.float32)[None, :])[:, :, None]
        rotated = rotate(amplitude, wavenumber).astype(jnp.bfloat16)
        product = jnp.einsum('ij,ejn->ein', basis_change.astype(jnp.float32), rotated.astype(jnp.float32))
        fresh = product.astype(jnp.bfloat16)
        return (fresh.astype(jnp.float32), fresh)
    initial = start_amps.astype(jnp.float32)
    final_state, boundary_amps = lax.scan(advance, initial, (thresholds, intersection))
    return boundary_amps
```

```python
import functools
import jax
import jax.numpy as jnp
from jax import lax
from jax.experimental import pallas as pl
from jax.experimental.pallas import tpu as pltpu
from jax.sharding import PartitionSpec as P


def passed_along(value, axis, steps):
    count = lax.axis_size(axis)
    leading, last = (max(0, -steps), min(count, count - steps))
    return lax.ppermute(value, axis, [(source, source + steps) for source in range(leading, last)])


def per_device_pipelined(start_amps, energies, thresholds, intersection):
    sectors = lax.axis_size("sec")
    sector_index = lax.axis_index("sec")
    groups = lax.axis_size("ch")
    energy_count = energies.shape[0]
    step_count = sectors + energy_count - 1
    row_count = intersection.shape[1]
    width_cols = start_amps.shape[2]
    half_cols = width_cols // 2
    col_width = half_cols // groups
    intersection_whole, thresholds_whole = (
        lax.all_gather(intersection, "ch", axis=1, tiled=True),
        lax.all_gather(thresholds, "ch", axis=1, tiled=True),
    )
    basis_change = intersection_whole[0]
    channel_thresholds = thresholds_whole[0].astype(jnp.float32)
    channel_count = basis_change.shape[0]
    paired = start_amps.reshape(energy_count, row_count, 2, half_cols)
    start_cols = lax.all_to_all(paired, "ch", split_axis=3, concat_axis=1, tiled=True)
    stored_init = jnp.zeros((energy_count, channel_count, 2, col_width), jnp.bfloat16)

    def multiply(flat):
        return jnp.dot(basis_change, flat, preferred_element_type=jnp.float32).astype(jnp.bfloat16)

    def skipped(flat):
        return jnp.zeros((channel_count, 2 * col_width), jnp.bfloat16)

    def step(step_index, state_pair):
        outgoing, stored = state_pair
        incoming = passed_along(outgoing, "sec", 1)
        energy_raw = step_index - sector_index
        active = (energy_raw >= 0) & (energy_raw < energy_count)
        energy_slot = jnp.clip(energy_raw, 0, energy_count - 1)
        initial = lax.dynamic_index_in_dim(start_cols, energy_slot, 0, keepdims=False)
        source = jnp.where(sector_index == 0, initial, incoming).astype(jnp.float32)
        wavenumber = jnp.sqrt(energies[energy_slot] - channel_thresholds)[:, None]
        values_part = source[:, 0, :]
        slopes_part = source[:, 1, :]
        cosine = jnp.cos(wavenumber)
        sine_term = jnp.sin(wavenumber)
        new_values = cosine * values_part + sine_term / wavenumber * slopes_part
        new_slopes = -wavenumber * sine_term * values_part + cosine * slopes_part
        rotated = jnp.stack([new_values, new_slopes], axis=1).astype(jnp.bfloat16)
        flat = rotated.reshape(channel_count, 2 * col_width)
        fresh = lax.cond(active, multiply, skipped, flat)
        fresh = fresh.reshape(channel_count, 2, col_width)
        previous = lax.dynamic_index_in_dim(stored, energy_slot, 0, keepdims=False)
        kept = jnp.where(active, fresh, previous)
        stored = lax.dynamic_update_index_in_dim(stored, kept, energy_slot, 0)
        return (fresh, stored)

    outgoing_init = jnp.zeros((channel_count, 2, col_width), jnp.bfloat16)
    final_pair = lax.fori_loop(0, step_count, step, (outgoing_init, stored_init))
    returned = lax.all_to_all(final_pair[1], "ch", split_axis=1, concat_axis=3, tiled=True)
    return returned.reshape(energy_count, row_count, width_cols)[None]


AUX_ROWS = 16
ROTATE_ROWS = 64


def sweep_kernel(
    sectors, groups, start, levels, own_block, out,
    basis, amps, rotated, kept, turn,
    local_sem, block_recv, spread_send, up_send, down_send, core_send,
    start_recv, start_up, start_down, out_send, out_recv, out_local,
):
    k = lax.axis_index("sec")
    z = lax.axis_index("ch")
    core = k % 2
    partner = k + 1 - 2 * core
    pairs = sectors // 2
    energy_count, row_count, width_cols = start.shape
    half_cols = width_cols // 2
    width = half_cols // sectors
    channel_count = row_count * groups
    has_up = z + 1 < groups
    has_down = z >= 1

    def remote(src, dst, send, recv, **where):
        return pltpu.make_async_remote_copy(
            src_ref=src, dst_ref=dst, send_sem=send, recv_sem=recv,
            device_id=where, device_id_type=pl.DeviceIdType.MESH,
        )

    def rows_of(c):
        return pl.ds(pl.multiple_of(c * row_count, row_count), row_count)

    def block_up(i, c):
        s = 2 * i + core
        return remote(basis.at[s, c], basis.at[s, c], up_send.at[i, c], block_recv.at[s, c], ch=z + 1)

    def block_down(i, c):
        s = 2 * i + core
        return remote(basis.at[s, c], basis.at[s, c], down_send.at[i, c], block_recv.at[s, c], ch=z - 1)

    def block_core(i, c):
        s = 2 * i + core
        return remote(basis.at[s, c], basis.at[s, c], core_send.at[i, c], block_recv.at[s, c], sec=partner)

    def block_spread(step):
        target = 2 * ((k // 2 + step) % pairs) + core
        return remote(basis.at[k, z], basis.at[k, z], spread_send.at[step], block_recv.at[k, z], sec=target)

    def block_arrived(s, c):
        remote(basis.at[s, c], basis.at[s, c], core_send.at[0, 0], block_recv.at[s, c], sec=partner).wait_recv()

    def start_part(e, c):
        return amps.at[0, e, rows_of(c), :]

    def start_move(e, c, send, **where):
        return remote(start_part(e, c), start_part(e, c), send.at[c], start_recv.at[e, c], **where)

    def start_arrived(e, c):
        remote(start_part(e, c), start_part(e, c), start_up.at[0], start_recv.at[e, c], sec=partner).wait_recv()

    loads = [
        pltpu.make_async_copy(own_block, basis.at[k, z], local_sem.at[0]),
        pltpu.make_async_copy(
            start.at[:, :, pl.ds(pl.multiple_of(k * width, width), width)],
            amps.at[0, :, rows_of(z), pl.ds(0, width)], local_sem.at[1]),
        pltpu.make_async_copy(
            start.at[:, :, pl.ds(pl.multiple_of(half_cols + k * width, width), width)],
            amps.at[0, :, rows_of(z), pl.ds(width, width)], local_sem.at[2]),
    ]
    for load in loads:
        load.start()

    barrier = pltpu.get_barrier_semaphore()
    for step in range(1, sectors):
        pl.semaphore_signal(barrier, inc=1, device_id={"sec": (k + step) % sectors}, device_id_type=pl.DeviceIdType.MESH)

    @pl.when(has_up)
    def _():
        pl.semaphore_signal(barrier, inc=1, device_id={"ch": z + 1}, device_id_type=pl.DeviceIdType.MESH)

    @pl.when(has_down)
    def _():
        pl.semaphore_signal(barrier, inc=1, device_id={"ch": z - 1}, device_id_type=pl.DeviceIdType.MESH)

    line_peers = jnp.minimum(z, 1) + jnp.minimum(groups - 1 - z, 1)
    pl.semaphore_wait(barrier, sectors - 1 + line_peers)
    for load in loads:
        load.wait()
    for step in range(1, pairs):
        block_spread(step).start()

    def each_energy(action):
        @pl.loop(0, energy_count)
        def _(e):
            action(e)

    @pl.when(has_up)
    def _():
        each_energy(lambda e: start_move(e, z, start_up, ch=z + 1).start())

    @pl.when(has_down)
    def _():
        each_energy(lambda e: start_move(e, z, start_down, ch=z - 1).start())

    def own_step(i):
        s = 2 * i + core

        @pl.when(s != k)
        def _():
            block_arrived(s, z)

        @pl.when(has_up)
        def _():
            block_up(i, z).start()

        @pl.when(has_down)
        def _():
            block_down(i, z).start()

        block_core(i, z).start()

    def forward_step(i, d):
        s = 2 * i + core

        @pl.when(z - d >= 0)
        def _():
            block_arrived(s, z - d)

            @pl.when(has_up)
            def _():
                block_up(i, z - d).start()

            block_core(i, z - d).start()

        @pl.when(z + d < groups)
        def _():
            block_arrived(s, z + d)

            @pl.when(has_down)
            def _():
                block_down(i, z + d).start()

            block_core(i, z + d).start()

    def start_forward(d):
        @pl.when(z - d >= 0)
        def _():
            def action(e):
                start_arrived(e, z - d)

                @pl.when(has_up)
                def _():
                    start_move(e, z - d, start_up, ch=z + 1).start()

            each_energy(action)

        @pl.when(z + d < groups)
        def _():
            def action(e):
                start_arrived(e, z + d)

                @pl.when(has_down)
                def _():
                    start_move(e, z + d, start_down, ch=z - 1).start()

            each_energy(action)

    own_step(0)
    for d in range(1, groups):
        start_forward(d)
        forward_step(0, d)

    def send_energy(s, e):
        for half in range(2):
            columns = pl.ds(pl.multiple_of(half * half_cols + k * width, width), width)

            @pl.when(s == k)
            def _():
                pltpu.make_async_copy(kept.at[s, half, e], out.at[e, :, columns], out_local.at[0]).start()

            @pl.when(s != k)
            def _():
                remote(kept.at[s, half, e], out.at[e, :, columns], out_send.at[s], out_recv.at[k], sec=s).start()

    def rotate(s):
        source = jnp.minimum(s, 1)

        @pl.loop(0, groups)
        def _(c):
            limits = basis[s, c, row_count:, :row_count].astype(jnp.float32)[0:1, :]
            wavenumber = jnp.sqrt(levels[...][:, 0:1] - limits)
            cosine = jnp.cos(wavenumber)
            sine_term = jnp.sin(wavenumber)
            rows = wavenumber.shape[0]
            filler = jnp.zeros((128 - 3 * rows, row_count), jnp.float32)
            stacked = jnp.concatenate(
                [cosine, sine_term / wavenumber, -wavenumber * sine_term, filler], axis=0
            )
            turn[...] = stacked.T

            @pl.loop(0, row_count // ROTATE_ROWS)
            def _(r):
                local = pl.ds(pl.multiple_of(r * ROTATE_ROWS, ROTATE_ROWS), ROTATE_ROWS)
                place = pl.ds(pl.multiple_of(c * row_count + r * ROTATE_ROWS, ROTATE_ROWS), ROTATE_ROWS)
                factors = turn[local, :]
                for e in range(energy_count):
                    both = amps[source, e, place, :].astype(jnp.float32)
                    values_part, slopes_part = both[:, :width], both[:, width:]
                    keep = factors[:, e : e + 1]
                    rise = factors[:, rows + e : rows + e + 1]
                    fall = factors[:, 2 * rows + e : 2 * rows + e + 1]
                    rotated[e, place, pl.ds(0, width)] = (keep * values_part + rise * slopes_part).astype(jnp.bfloat16)
                    rotated[e, place, pl.ds(width, width)] = (fall * values_part + keep * slopes_part).astype(jnp.bfloat16)

    def multiply(s):
        @pl.loop(0, energy_count)
        def _(e):
            @pl.loop(0, groups)
            def _(c):
                @pl.when((s < sectors - 1) | (c == z))
                def _():
                    product = jnp.dot(
                        basis[s, c, :row_count, :], rotated[e], preferred_element_type=jnp.float32
                    ).astype(jnp.bfloat16)
                    amps[1, e, rows_of(c), :] = product

                    @pl.when(c == z)
                    def _():
                        kept[s, 0, e] = product[:, :width]
                        kept[s, 1, e] = product[:, width:]

            @pl.when(e >= 1)
            def _():
                send_energy(s, e - 1)

    @pl.loop(0, pairs)
    def _(i):
        more = i + 1 < pairs

        @pl.when(more)
        def _():
            own_step(i + 1)

        for c in range(groups):
            block_arrived(2 * i + 1 - core, c)
        rotate(2 * i)

        @pl.when(i >= 1)
        def _():
            send_energy(2 * i - 1, energy_count - 1)

        multiply(2 * i)

        @pl.when(more)
        def _():
            for d in range(1, groups - 1):
                forward_step(i + 1, d)

        rotate(2 * i + 1)
        send_energy(2 * i, energy_count - 1)
        multiply(2 * i + 1)

        @pl.when(more)
        def _():
            forward_step(i + 1, groups - 1)

    for step in range(1, pairs):
        block_spread(step).wait_send()

    @pl.loop(0, pairs)
    def _(i):
        for c in range(groups):
            block_core(i, c).wait_send()

            @pl.when(has_up & (c <= z))
            def _():
                block_up(i, c).wait_send()

            @pl.when(has_down & (c >= z))
            def _():
                block_down(i, c).wait_send()

    for c in range(groups):
        span = amps.at[0, :, pl.ds(c * row_count, row_count), :]

        @pl.when(has_up & (c <= z))
        def _():
            remote(span, span, start_up.at[c], start_recv.at[0, 0], ch=z + 1).wait_send()

        @pl.when(has_down & (c >= z))
        def _():
            remote(span, span, start_down.at[c], start_recv.at[0, 0], ch=z - 1).wait_send()

    send_energy(sectors - 1, energy_count - 1)

    @pl.loop(0, sectors)
    def _(s):
        whole = remote(kept.at[s], kept.at[s], out_send.at[s], out_recv.at[s], sec=partner)

        @pl.when(s != k)
        def _():
            whole.wait_send()
            whole.wait_recv()

        @pl.when(s == k)
        def _():
            pltpu.make_async_copy(kept.at[s], kept.at[s], out_local.at[0]).wait()


def per_device_swept(start_amps, energies, thresholds, intersection):
    sectors = lax.axis_size("sec")
    groups = lax.axis_size("ch")
    energy_count, row_count, width_cols = start_amps.shape
    channel_count = intersection.shape[2]
    width = width_cols // 2 // sectors
    pairs = sectors // 2
    padded = jnp.concatenate([energies, jnp.broadcast_to(energies[:1], (-energy_count % 8,))])
    levels = jnp.broadcast_to(padded[:, None], (padded.shape[0], 128))
    aux = jnp.pad(thresholds, ((0, AUX_ROWS - 1), (0, channel_count - row_count)))
    own_block = jnp.concatenate([intersection[0], aux], axis=0)
    dma = pltpu.SemaphoreType.DMA
    stored = jax.ShapeDtypeStruct(start_amps.shape, jnp.bfloat16)
    swept = pl.pallas_call(
        functools.partial(sweep_kernel, sectors, groups),
        out_shape=stored,
        in_specs=[
            pl.BlockSpec(memory_space=pl.ANY),
            pl.BlockSpec(memory_space=pltpu.VMEM),
            pl.BlockSpec(memory_space=pl.ANY),
        ],
        out_specs=pl.BlockSpec(memory_space=pl.ANY),
        scratch_shapes=[
            pltpu.VMEM((sectors, groups, row_count + AUX_ROWS, channel_count), jnp.bfloat16),
            pltpu.VMEM((2, energy_count, channel_count, 2 * width), jnp.bfloat16),
            pltpu.VMEM((energy_count, channel_count, 2 * width), jnp.bfloat16),
            pltpu.VMEM((sectors, 2, energy_count, row_count, width), jnp.bfloat16),
            pltpu.VMEM((row_count, 128), jnp.float32),
            dma((3,)),
            dma((sectors, groups)),
            dma((pairs,)),
            dma((pairs, groups)),
            dma((pairs, groups)),
            dma((pairs, groups)),
            dma((energy_count, groups)),
            dma((groups,)),
            dma((groups,)),
            dma((sectors,)),
            dma((sectors,)),
            dma((1,)),
        ],
        compiler_params=pltpu.CompilerParams(
            collective_id=0, has_side_effects=True, vmem_limit_bytes=60 * 2**20
        ),
    )(start_amps, levels, own_block)
    return swept[None]


GATHERED_LIMIT = 24 * 2**20


def per_device(start_amps, energies, thresholds, intersection):
    sectors = lax.axis_size("sec")
    row_count, channel_count = intersection.shape[1:]
    gathered_bytes = sectors * channel_count**2 * intersection.dtype.itemsize
    even = sectors % 2 == 0 and (start_amps.shape[2] // 2) % (sectors * 128) == 0
    even = even and row_count % 128 == 0 and energies.shape[0] <= 40
    if even and gathered_bytes <= GATHERED_LIMIT:
        return per_device_swept(start_amps, energies, thresholds, intersection)
    return per_device_pipelined(start_amps, energies, thresholds, intersection)


def solution(mesh):
    in_specs = (P(None, "ch", None), P(), P("sec", "ch"), P("sec", "ch", None))
    out_specs = P("sec", None, "ch", None)
    return jax.shard_map(
        per_device, mesh=mesh, in_specs=in_specs, out_specs=out_specs, check_vma=False
    )
```

```python
import functools
import jax
import jax.numpy as jnp
from jax import lax
from jax.experimental import pallas as pl
from jax.experimental.pallas import tpu as pltpu
from jax.sharding import PartitionSpec as P


def passed_along(value, axis, steps):
    count = lax.axis_size(axis)
    leading, last = (max(0, -steps), min(count, count - steps))
    return lax.ppermute(value, axis, [(source, source + steps) for source in range(leading, last)])


def per_device_pipelined(start_amps, energies, thresholds, intersection):
    sectors = lax.axis_size("sec")
    sector_index = lax.axis_index("sec")
    groups = lax.axis_size("ch")
    energy_count = energies.shape[0]
    step_count = sectors + energy_count - 1
    row_count = intersection.shape[1]
    width_cols = start_amps.shape[2]
    half_cols = width_cols // 2
    col_width = half_cols // groups
    intersection_whole, thresholds_whole = (
        lax.all_gather(intersection, "ch", axis=1, tiled=True),
        lax.all_gather(thresholds, "ch", axis=1, tiled=True),
    )
    basis_change = intersection_whole[0]
    channel_thresholds = thresholds_whole[0].astype(jnp.float32)
    channel_count = basis_change.shape[0]
    paired = start_amps.reshape(energy_count, row_count, 2, half_cols)
    start_cols = lax.all_to_all(paired, "ch", split_axis=3, concat_axis=1, tiled=True)
    stored_init = jnp.zeros((energy_count, channel_count, 2, col_width), jnp.bfloat16)

    def multiply(flat):
        return jnp.dot(basis_change, flat, preferred_element_type=jnp.float32).astype(jnp.bfloat16)

    def skipped(flat):
        return jnp.zeros((channel_count, 2 * col_width), jnp.bfloat16)

    def step(step_index, state_pair):
        outgoing, stored = state_pair
        incoming = passed_along(outgoing, "sec", 1)
        energy_raw = step_index - sector_index
        active = (energy_raw >= 0) & (energy_raw < energy_count)
        energy_slot = jnp.clip(energy_raw, 0, energy_count - 1)
        initial = lax.dynamic_index_in_dim(start_cols, energy_slot, 0, keepdims=False)
        source = jnp.where(sector_index == 0, initial, incoming).astype(jnp.float32)
        wavenumber = jnp.sqrt(energies[energy_slot] - channel_thresholds)[:, None]
        values_part = source[:, 0, :]
        slopes_part = source[:, 1, :]
        cosine = jnp.cos(wavenumber)
        sine_term = jnp.sin(wavenumber)
        new_values = cosine * values_part + sine_term / wavenumber * slopes_part
        new_slopes = -wavenumber * sine_term * values_part + cosine * slopes_part
        rotated = jnp.stack([new_values, new_slopes], axis=1).astype(jnp.bfloat16)
        flat = rotated.reshape(channel_count, 2 * col_width)
        fresh = lax.cond(active, multiply, skipped, flat)
        fresh = fresh.reshape(channel_count, 2, col_width)
        previous = lax.dynamic_index_in_dim(stored, energy_slot, 0, keepdims=False)
        kept = jnp.where(active, fresh, previous)
        stored = lax.dynamic_update_index_in_dim(stored, kept, energy_slot, 0)
        return (fresh, stored)

    outgoing_init = jnp.zeros((channel_count, 2, col_width), jnp.bfloat16)
    final_pair = lax.fori_loop(0, step_count, step, (outgoing_init, stored_init))
    returned = lax.all_to_all(final_pair[1], "ch", split_axis=1, concat_axis=3, tiled=True)
    return returned.reshape(energy_count, row_count, width_cols)[None]


AUX_ROWS = 16
ROTATE_ROWS = 64


def sweep_kernel(
    sectors, groups, start, levels, own_block, out,
    basis, amps, rotated, kept, turn,
    local_sem, block_recv, spread_send, up_send, down_send, core_send,
    start_recv, start_up, start_down, out_send, out_recv, out_local,
):
    k = lax.axis_index("sec")
    z = lax.axis_index("ch")
    core = k % 2
    partner = k + 1 - 2 * core
    pairs = sectors // 2
    energy_count, row_count, width_cols = start.shape
    half_cols = width_cols // 2
    width = half_cols // sectors
    channel_count = row_count * groups
    has_up = z + 1 < groups
    has_down = z >= 1

    def remote(src, dst, send, recv, **where):
        return pltpu.make_async_remote_copy(
            src_ref=src, dst_ref=dst, send_sem=send, recv_sem=recv,
            device_id=where, device_id_type=pl.DeviceIdType.MESH,
        )

    def rows_of(c):
        return pl.ds(pl.multiple_of(c * row_count, row_count), row_count)

    def block_up(i, c):
        s = 2 * i + core
        return remote(basis.at[s, c], basis.at[s, c], up_send.at[i, c], block_recv.at[s, c], ch=z + 1)

    def block_down(i, c):
        s = 2 * i + core
        return remote(basis.at[s, c], basis.at[s, c], down_send.at[i, c], block_recv.at[s, c], ch=z - 1)

    def block_core(i, c):
        s = 2 * i + core
        return remote(basis.at[s, c], basis.at[s, c], core_send.at[i, c], block_recv.at[s, c], sec=partner)

    def block_spread(step):
        target = 2 * ((k // 2 + step) % pairs) + core
        return remote(basis.at[k, z], basis.at[k, z], spread_send.at[step], block_recv.at[k, z], sec=target)

    def block_arrived(s, c):
        remote(basis.at[s, c], basis.at[s, c], core_send.at[0, 0], block_recv.at[s, c], sec=partner).wait_recv()

    def start_part(e, c):
        return amps.at[0, e, rows_of(c), :]

    def start_move(e, c, send, **where):
        return remote(start_part(e, c), start_part(e, c), send.at[c], start_recv.at[e, c], **where)

    def start_arrived(e, c):
        remote(start_part(e, c), start_part(e, c), start_up.at[0], start_recv.at[e, c], sec=partner).wait_recv()

    loads = [
        pltpu.make_async_copy(own_block, basis.at[k, z], local_sem.at[0]),
        pltpu.make_async_copy(
            start.at[:, :, pl.ds(pl.multiple_of(k * width, width), width)],
            amps.at[0, :, rows_of(z), pl.ds(0, width)], local_sem.at[1]),
        pltpu.make_async_copy(
            start.at[:, :, pl.ds(pl.multiple_of(half_cols + k * width, width), width)],
            amps.at[0, :, rows_of(z), pl.ds(width, width)], local_sem.at[2]),
    ]
    for load in loads:
        load.start()

    barrier = pltpu.get_barrier_semaphore()
    for step in range(1, sectors):
        pl.semaphore_signal(barrier, inc=1, device_id={"sec": (k + step) % sectors}, device_id_type=pl.DeviceIdType.MESH)

    @pl.when(has_up)
    def _():
        pl.semaphore_signal(barrier, inc=1, device_id={"ch": z + 1}, device_id_type=pl.DeviceIdType.MESH)

    @pl.when(has_down)
    def _():
        pl.semaphore_signal(barrier, inc=1, device_id={"ch": z - 1}, device_id_type=pl.DeviceIdType.MESH)

    line_peers = jnp.minimum(z, 1) + jnp.minimum(groups - 1 - z, 1)
    pl.semaphore_wait(barrier, sectors - 1 + line_peers)
    for load in loads:
        load.wait()
    for step in range(1, pairs):
        block_spread(step).start()

    def each_energy(action):
        @pl.loop(0, energy_count)
        def _(e):
            action(e)

    @pl.when(has_up)
    def _():
        each_energy(lambda e: start_move(e, z, start_up, ch=z + 1).start())

    @pl.when(has_down)
    def _():
        each_energy(lambda e: start_move(e, z, start_down, ch=z - 1).start())

    def own_step(i):
        s = 2 * i + core

        @pl.when(s != k)
        def _():
            block_arrived(s, z)

        @pl.when(has_up)
        def _():
            block_up(i, z).start()

        @pl.when(has_down)
        def _():
            block_down(i, z).start()

        block_core(i, z).start()

    def forward_step(i, d):
        s = 2 * i + core

        @pl.when(z - d >= 0)
        def _():
            block_arrived(s, z - d)

            @pl.when(has_up)
            def _():
                block_up(i, z - d).start()

            block_core(i, z - d).start()

        @pl.when(z + d < groups)
        def _():
            block_arrived(s, z + d)

            @pl.when(has_down)
            def _():
                block_down(i, z + d).start()

            block_core(i, z + d).start()

    def start_forward(d):
        @pl.when(z - d >= 0)
        def _():
            def action(e):
                start_arrived(e, z - d)

                @pl.when(has_up)
                def _():
                    start_move(e, z - d, start_up, ch=z + 1).start()

            each_energy(action)

        @pl.when(z + d < groups)
        def _():
            def action(e):
                start_arrived(e, z + d)

                @pl.when(has_down)
                def _():
                    start_move(e, z + d, start_down, ch=z - 1).start()

            each_energy(action)

    lag = max(groups // 2, 1)
    own_step(0)
    for d in range(1, groups):
        start_forward(d)
        forward_step(0, d)
        if pairs > 1 and d == lag:
            own_step(1)
        if pairs > 1 and d > lag:
            forward_step(1, d - lag)

    def send_energy(s, e):
        for half in range(2):
            columns = pl.ds(pl.multiple_of(half * half_cols + k * width, width), width)

            @pl.when(s == k)
            def _():
                pltpu.make_async_copy(kept.at[s, half, e], out.at[e, :, columns], out_local.at[0]).start()

            @pl.when(s != k)
            def _():
                remote(kept.at[s, half, e], out.at[e, :, columns], out_send.at[s], out_recv.at[k], sec=s).start()

    def rotate(s):
        source = jnp.minimum(s, 1)

        @pl.loop(0, groups)
        def _(c):
            limits = basis[s, c, row_count:, :row_count].astype(jnp.float32)[0:1, :]
            wavenumber = jnp.sqrt(levels[...][:, 0:1] - limits)
            cosine = jnp.cos(wavenumber)
            sine_term = jnp.sin(wavenumber)
            rows = wavenumber.shape[0]
            filler = jnp.zeros((128 - 3 * rows, row_count), jnp.float32)
            stacked = jnp.concatenate(
                [cosine, sine_term / wavenumber, -wavenumber * sine_term, filler], axis=0
            )
            turn[...] = stacked.T

            @pl.loop(0, row_count // ROTATE_ROWS)
            def _(r):
                local = pl.ds(pl.multiple_of(r * ROTATE_ROWS, ROTATE_ROWS), ROTATE_ROWS)
                place = pl.ds(pl.multiple_of(c * row_count + r * ROTATE_ROWS, ROTATE_ROWS), ROTATE_ROWS)
                factors = turn[local, :]
                for e in range(energy_count):
                    both = amps[source, e, place, :].astype(jnp.float32)
                    values_part, slopes_part = both[:, :width], both[:, width:]
                    keep = factors[:, e : e + 1]
                    rise = factors[:, rows + e : rows + e + 1]
                    fall = factors[:, 2 * rows + e : 2 * rows + e + 1]
                    rotated[e, place, pl.ds(0, width)] = (keep * values_part + rise * slopes_part).astype(jnp.bfloat16)
                    rotated[e, place, pl.ds(width, width)] = (fall * values_part + keep * slopes_part).astype(jnp.bfloat16)

    def multiply(s):
        @pl.loop(0, energy_count)
        def _(e):
            @pl.loop(0, groups)
            def _(c):
                @pl.when((s < sectors - 1) | (c == z))
                def _():
                    product = jnp.dot(
                        basis[s, c, :row_count, :], rotated[e], preferred_element_type=jnp.float32
                    ).astype(jnp.bfloat16)
                    amps[1, e, rows_of(c), :] = product

                    @pl.when(c == z)
                    def _():
                        kept[s, 0, e] = product[:, :width]
                        kept[s, 1, e] = product[:, width:]

            @pl.when(e >= 1)
            def _():
                send_energy(s, e - 1)

    @pl.loop(0, pairs)
    def _(i):
        more = i + 1 < pairs
        further = i + 2 < pairs

        @pl.when(further)
        def _():
            own_step(i + 2)

        for c in range(groups):
            block_arrived(2 * i + 1 - core, c)
        rotate(2 * i)

        @pl.when(i >= 1)
        def _():
            send_energy(2 * i - 1, energy_count - 1)

        multiply(2 * i)

        @pl.when(more)
        def _():
            for d in range(max(groups - lag, 1), groups - 1):
                forward_step(i + 1, d)

        rotate(2 * i + 1)
        send_energy(2 * i, energy_count - 1)
        multiply(2 * i + 1)

        @pl.when(more)
        def _():
            forward_step(i + 1, groups - 1)

        @pl.when(further)
        def _():
            for d in range(1, groups - lag):
                forward_step(i + 2, d)

    for step in range(1, pairs):
        block_spread(step).wait_send()

    @pl.loop(0, pairs)
    def _(i):
        for c in range(groups):
            block_core(i, c).wait_send()

            @pl.when(has_up & (c <= z))
            def _():
                block_up(i, c).wait_send()

            @pl.when(has_down & (c >= z))
            def _():
                block_down(i, c).wait_send()

    for c in range(groups):
        span = amps.at[0, :, pl.ds(c * row_count, row_count), :]

        @pl.when(has_up & (c <= z))
        def _():
            remote(span, span, start_up.at[c], start_recv.at[0, 0], ch=z + 1).wait_send()

        @pl.when(has_down & (c >= z))
        def _():
            remote(span, span, start_down.at[c], start_recv.at[0, 0], ch=z - 1).wait_send()

    send_energy(sectors - 1, energy_count - 1)

    @pl.loop(0, sectors)
    def _(s):
        whole = remote(kept.at[s], kept.at[s], out_send.at[s], out_recv.at[s], sec=partner)

        @pl.when(s != k)
        def _():
            whole.wait_send()
            whole.wait_recv()

        @pl.when(s == k)
        def _():
            pltpu.make_async_copy(kept.at[s], kept.at[s], out_local.at[0]).wait()


def per_device_swept(start_amps, energies, thresholds, intersection):
    sectors = lax.axis_size("sec")
    groups = lax.axis_size("ch")
    energy_count, row_count, width_cols = start_amps.shape
    channel_count = intersection.shape[2]
    width = width_cols // 2 // sectors
    pairs = sectors // 2
    padded = jnp.concatenate([energies, jnp.broadcast_to(energies[:1], (-energy_count % 8,))])
    levels = jnp.broadcast_to(padded[:, None], (padded.shape[0], 128))
    aux = jnp.pad(thresholds, ((0, AUX_ROWS - 1), (0, channel_count - row_count)))
    own_block = jnp.concatenate([intersection[0], aux], axis=0)
    dma = pltpu.SemaphoreType.DMA
    stored = jax.ShapeDtypeStruct(start_amps.shape, jnp.bfloat16)
    swept = pl.pallas_call(
        functools.partial(sweep_kernel, sectors, groups),
        out_shape=stored,
        in_specs=[
            pl.BlockSpec(memory_space=pl.ANY),
            pl.BlockSpec(memory_space=pltpu.VMEM),
            pl.BlockSpec(memory_space=pl.ANY),
        ],
        out_specs=pl.BlockSpec(memory_space=pl.ANY),
        scratch_shapes=[
            pltpu.VMEM((sectors, groups, row_count + AUX_ROWS, channel_count), jnp.bfloat16),
            pltpu.VMEM((2, energy_count, channel_count, 2 * width), jnp.bfloat16),
            pltpu.VMEM((energy_count, channel_count, 2 * width), jnp.bfloat16),
            pltpu.VMEM((sectors, 2, energy_count, row_count, width), jnp.bfloat16),
            pltpu.VMEM((row_count, 128), jnp.float32),
            dma((3,)),
            dma((sectors, groups)),
            dma((pairs,)),
            dma((pairs, groups)),
            dma((pairs, groups)),
            dma((pairs, groups)),
            dma((energy_count, groups)),
            dma((groups,)),
            dma((groups,)),
            dma((sectors,)),
            dma((sectors,)),
            dma((1,)),
        ],
        compiler_params=pltpu.CompilerParams(
            collective_id=0, has_side_effects=True, vmem_limit_bytes=60 * 2**20
        ),
    )(start_amps, levels, own_block)
    return swept[None]


GATHERED_LIMIT = 24 * 2**20


def per_device(start_amps, energies, thresholds, intersection):
    sectors = lax.axis_size("sec")
    row_count, channel_count = intersection.shape[1:]
    gathered_bytes = sectors * channel_count**2 * intersection.dtype.itemsize
    even = sectors % 2 == 0 and (start_amps.shape[2] // 2) % (sectors * 128) == 0
    even = even and row_count % 128 == 0 and energies.shape[0] <= 40
    if even and gathered_bytes <= GATHERED_LIMIT:
        return per_device_swept(start_amps, energies, thresholds, intersection)
    return per_device_pipelined(start_amps, energies, thresholds, intersection)


def solution(mesh):
    in_specs = (P(None, "ch", None), P(), P("sec", "ch"), P("sec", "ch", None))
    out_specs = P("sec", None, "ch", None)
    return jax.shard_map(
        per_device, mesh=mesh, in_specs=in_specs, out_specs=out_specs, check_vma=False
    )
```

```python
import functools
import jax
import jax.numpy as jnp
from jax import lax
from jax.experimental import pallas as pl
from jax.experimental.pallas import tpu as pltpu
from jax.sharding import PartitionSpec as P


def passed_along(value, axis, steps):
    count = lax.axis_size(axis)
    leading, last = (max(0, -steps), min(count, count - steps))
    return lax.ppermute(value, axis, [(source, source + steps) for source in range(leading, last)])


def per_device_pipelined(start_amps, energies, thresholds, intersection):
    sectors = lax.axis_size("sec")
    sector_index = lax.axis_index("sec")
    groups = lax.axis_size("ch")
    energy_count = energies.shape[0]
    step_count = sectors + energy_count - 1
    row_count = intersection.shape[1]
    width_cols = start_amps.shape[2]
    half_cols = width_cols // 2
    col_width = half_cols // groups
    intersection_whole, thresholds_whole = (
        lax.all_gather(intersection, "ch", axis=1, tiled=True),
        lax.all_gather(thresholds, "ch", axis=1, tiled=True),
    )
    basis_change = intersection_whole[0]
    channel_thresholds = thresholds_whole[0].astype(jnp.float32)
    channel_count = basis_change.shape[0]
    paired = start_amps.reshape(energy_count, row_count, 2, half_cols)
    start_cols = lax.all_to_all(paired, "ch", split_axis=3, concat_axis=1, tiled=True)
    stored_init = jnp.zeros((energy_count, channel_count, 2, col_width), jnp.bfloat16)

    def multiply(flat):
        return jnp.dot(basis_change, flat, preferred_element_type=jnp.float32).astype(jnp.bfloat16)

    def skipped(flat):
        return jnp.zeros((channel_count, 2 * col_width), jnp.bfloat16)

    def step(step_index, state_pair):
        outgoing, stored = state_pair
        incoming = passed_along(outgoing, "sec", 1)
        energy_raw = step_index - sector_index
        active = (energy_raw >= 0) & (energy_raw < energy_count)
        energy_slot = jnp.clip(energy_raw, 0, energy_count - 1)
        initial = lax.dynamic_index_in_dim(start_cols, energy_slot, 0, keepdims=False)
        source = jnp.where(sector_index == 0, initial, incoming).astype(jnp.float32)
        wavenumber = jnp.sqrt(energies[energy_slot] - channel_thresholds)[:, None]
        values_part = source[:, 0, :]
        slopes_part = source[:, 1, :]
        cosine = jnp.cos(wavenumber)
        sine_term = jnp.sin(wavenumber)
        new_values = cosine * values_part + sine_term / wavenumber * slopes_part
        new_slopes = -wavenumber * sine_term * values_part + cosine * slopes_part
        rotated = jnp.stack([new_values, new_slopes], axis=1).astype(jnp.bfloat16)
        flat = rotated.reshape(channel_count, 2 * col_width)
        fresh = lax.cond(active, multiply, skipped, flat)
        fresh = fresh.reshape(channel_count, 2, col_width)
        previous = lax.dynamic_index_in_dim(stored, energy_slot, 0, keepdims=False)
        kept = jnp.where(active, fresh, previous)
        stored = lax.dynamic_update_index_in_dim(stored, kept, energy_slot, 0)
        return (fresh, stored)

    outgoing_init = jnp.zeros((channel_count, 2, col_width), jnp.bfloat16)
    final_pair = lax.fori_loop(0, step_count, step, (outgoing_init, stored_init))
    returned = lax.all_to_all(final_pair[1], "ch", split_axis=1, concat_axis=3, tiled=True)
    return returned.reshape(energy_count, row_count, width_cols)[None]


AUX_ROWS = 16
ROTATE_ROWS = 64


def sweep_kernel(
    sectors, groups, start, levels, own_block, out,
    basis, amps, rotated, kept, turn,
    local_sem, block_recv, spread_send, up_send, down_send, core_send,
    start_recv, start_up, start_down, out_send, out_recv, out_local,
):
    k = lax.axis_index("sec")
    z = lax.axis_index("ch")
    core = k % 2
    partner = k + 1 - 2 * core
    pairs = sectors // 2
    energy_count, row_count, width_cols = start.shape
    half_cols = width_cols // 2
    width = half_cols // sectors
    channel_count = row_count * groups
    has_up = z + 1 < groups
    has_down = z >= 1

    def remote(src, dst, send, recv, **where):
        return pltpu.make_async_remote_copy(
            src_ref=src, dst_ref=dst, send_sem=send, recv_sem=recv,
            device_id=where, device_id_type=pl.DeviceIdType.MESH,
        )

    def rows_of(c):
        return pl.ds(pl.multiple_of(c * row_count, row_count), row_count)

    def block_up(i, c):
        s = 2 * i + core
        return remote(basis.at[s, c], basis.at[s, c], up_send.at[i, c], block_recv.at[s, c], ch=z + 1)

    def block_down(i, c):
        s = 2 * i + core
        return remote(basis.at[s, c], basis.at[s, c], down_send.at[i, c], block_recv.at[s, c], ch=z - 1)

    def block_core(i, c):
        s = 2 * i + core
        return remote(basis.at[s, c], basis.at[s, c], core_send.at[i, c], block_recv.at[s, c], sec=partner)

    def block_spread(step):
        target = 2 * ((k // 2 + step) % pairs) + core
        return remote(basis.at[k, z], basis.at[k, z], spread_send.at[step], block_recv.at[k, z], sec=target)

    def block_arrived(s, c):
        remote(basis.at[s, c], basis.at[s, c], core_send.at[0, 0], block_recv.at[s, c], sec=partner).wait_recv()

    def start_part(e, c):
        return amps.at[0, e, rows_of(c), :]

    def start_move(e, c, send, **where):
        return remote(start_part(e, c), start_part(e, c), send.at[c], start_recv.at[e, c], **where)

    def start_arrived(e, c):
        remote(start_part(e, c), start_part(e, c), start_up.at[0], start_recv.at[e, c], sec=partner).wait_recv()

    loads = [
        pltpu.make_async_copy(own_block, basis.at[k, z], local_sem.at[0]),
        pltpu.make_async_copy(
            start.at[:, :, pl.ds(pl.multiple_of(k * width, width), width)],
            amps.at[0, :, rows_of(z), pl.ds(0, width)], local_sem.at[1]),
        pltpu.make_async_copy(
            start.at[:, :, pl.ds(pl.multiple_of(half_cols + k * width, width), width)],
            amps.at[0, :, rows_of(z), pl.ds(width, width)], local_sem.at[2]),
    ]
    for load in loads:
        load.start()

    barrier = pltpu.get_barrier_semaphore()
    for step in range(1, sectors):
        pl.semaphore_signal(barrier, inc=1, device_id={"sec": (k + step) % sectors}, device_id_type=pl.DeviceIdType.MESH)

    @pl.when(has_up)
    def _():
        pl.semaphore_signal(barrier, inc=1, device_id={"ch": z + 1}, device_id_type=pl.DeviceIdType.MESH)

    @pl.when(has_down)
    def _():
        pl.semaphore_signal(barrier, inc=1, device_id={"ch": z - 1}, device_id_type=pl.DeviceIdType.MESH)

    line_peers = jnp.minimum(z, 1) + jnp.minimum(groups - 1 - z, 1)
    pl.semaphore_wait(barrier, sectors - 1 + line_peers)
    for load in loads:
        load.wait()
    for step in range(1, pairs):
        block_spread(step).start()

    def each_energy(action):
        @pl.loop(0, energy_count)
        def _(e):
            action(e)

    @pl.when(has_up)
    def _():
        each_energy(lambda e: start_move(e, z, start_up, ch=z + 1).start())

    @pl.when(has_down)
    def _():
        each_energy(lambda e: start_move(e, z, start_down, ch=z - 1).start())

    def own_step(i):
        s = 2 * i + core

        @pl.when(s != k)
        def _():
            block_arrived(s, z)

        @pl.when(has_up)
        def _():
            block_up(i, z).start()

        @pl.when(has_down)
        def _():
            block_down(i, z).start()

        block_core(i, z).start()

    def forward_step(i, d):
        s = 2 * i + core

        @pl.when(z - d >= 0)
        def _():
            block_arrived(s, z - d)

            @pl.when(has_up)
            def _():
                block_up(i, z - d).start()

            block_core(i, z - d).start()

        @pl.when(z + d < groups)
        def _():
            block_arrived(s, z + d)

            @pl.when(has_down)
            def _():
                block_down(i, z + d).start()

            block_core(i, z + d).start()

    def start_forward(d):
        @pl.when(z - d >= 0)
        def _():
            def action(e):
                start_arrived(e, z - d)

                @pl.when(has_up)
                def _():
                    start_move(e, z - d, start_up, ch=z + 1).start()

            each_energy(action)

        @pl.when(z + d < groups)
        def _():
            def action(e):
                start_arrived(e, z + d)

                @pl.when(has_down)
                def _():
                    start_move(e, z + d, start_down, ch=z - 1).start()

            each_energy(action)

    lag = max(groups // 2, 1)
    for i in range(min(pairs, 2)):
        own_step(i)
    for d in range(1, groups):
        start_forward(d)
        forward_step(0, d)
        if pairs > 2 and d == 1:
            own_step(2)
        if pairs > 1 and d > lag:
            forward_step(1, d - lag)

    def send_energy(s, e):
        for half in range(2):
            columns = pl.ds(pl.multiple_of(half * half_cols + k * width, width), width)

            @pl.when(s == k)
            def _():
                pltpu.make_async_copy(kept.at[s, half, e], out.at[e, :, columns], out_local.at[0]).start()

            @pl.when(s != k)
            def _():
                remote(kept.at[s, half, e], out.at[e, :, columns], out_send.at[s], out_recv.at[k], sec=s).start()

    def rotate(s):
        source = jnp.minimum(s, 1)

        @pl.loop(0, groups)
        def _(c):
            limits = basis[s, c, row_count:, :row_count].astype(jnp.float32)[0:1, :]
            wavenumber = jnp.sqrt(levels[...][:, 0:1] - limits)
            cosine = jnp.cos(wavenumber)
            sine_term = jnp.sin(wavenumber)
            rows = wavenumber.shape[0]
            filler = jnp.zeros((128 - 3 * rows, row_count), jnp.float32)
            stacked = jnp.concatenate(
                [cosine, sine_term / wavenumber, -wavenumber * sine_term, filler], axis=0
            )
            turn[...] = stacked.T

            @pl.loop(0, row_count // ROTATE_ROWS)
            def _(r):
                local = pl.ds(pl.multiple_of(r * ROTATE_ROWS, ROTATE_ROWS), ROTATE_ROWS)
                place = pl.ds(pl.multiple_of(c * row_count + r * ROTATE_ROWS, ROTATE_ROWS), ROTATE_ROWS)
                factors = turn[local, :]
                for e in range(energy_count):
                    both = amps[source, e, place, :].astype(jnp.float32)
                    values_part, slopes_part = both[:, :width], both[:, width:]
                    keep = factors[:, e : e + 1]
                    rise = factors[:, rows + e : rows + e + 1]
                    fall = factors[:, 2 * rows + e : 2 * rows + e + 1]
                    rotated[e, place, pl.ds(0, width)] = (keep * values_part + rise * slopes_part).astype(jnp.bfloat16)
                    rotated[e, place, pl.ds(width, width)] = (fall * values_part + keep * slopes_part).astype(jnp.bfloat16)

    def multiply(s):
        @pl.loop(0, energy_count)
        def _(e):
            @pl.loop(0, groups)
            def _(c):
                @pl.when((s < sectors - 1) | (c == z))
                def _():
                    product = jnp.dot(
                        basis[s, c, :row_count, :], rotated[e], preferred_element_type=jnp.float32
                    ).astype(jnp.bfloat16)
                    amps[1, e, rows_of(c), :] = product

                    @pl.when(c == z)
                    def _():
                        kept[s, 0, e] = product[:, :width]
                        kept[s, 1, e] = product[:, width:]

            @pl.when(e >= 1)
            def _():
                send_energy(s, e - 1)

    @pl.loop(0, pairs)
    def _(i):
        more = i + 1 < pairs
        further = i + 2 < pairs

        @pl.when(i + 3 < pairs)
        def _():
            own_step(i + 3)

        for c in range(groups):
            block_arrived(2 * i + 1 - core, c)
        rotate(2 * i)

        @pl.when(i >= 1)
        def _():
            send_energy(2 * i - 1, energy_count - 1)

        multiply(2 * i)

        @pl.when(more)
        def _():
            for d in range(max(groups - lag, 1), groups - 1):
                forward_step(i + 1, d)

        rotate(2 * i + 1)
        send_energy(2 * i, energy_count - 1)
        multiply(2 * i + 1)

        @pl.when(more)
        def _():
            forward_step(i + 1, groups - 1)

        @pl.when(further)
        def _():
            for d in range(1, groups - lag):
                forward_step(i + 2, d)

    for step in range(1, pairs):
        block_spread(step).wait_send()

    @pl.loop(0, pairs)
    def _(i):
        for c in range(groups):
            block_core(i, c).wait_send()

            @pl.when(has_up & (c <= z))
            def _():
                block_up(i, c).wait_send()

            @pl.when(has_down & (c >= z))
            def _():
                block_down(i, c).wait_send()

    for c in range(groups):
        span = amps.at[0, :, pl.ds(c * row_count, row_count), :]

        @pl.when(has_up & (c <= z))
        def _():
            remote(span, span, start_up.at[c], start_recv.at[0, 0], ch=z + 1).wait_send()

        @pl.when(has_down & (c >= z))
        def _():
            remote(span, span, start_down.at[c], start_recv.at[0, 0], ch=z - 1).wait_send()

    send_energy(sectors - 1, energy_count - 1)

    @pl.loop(0, sectors)
    def _(s):
        whole = remote(kept.at[s], kept.at[s], out_send.at[s], out_recv.at[s], sec=partner)

        @pl.when(s != k)
        def _():
            whole.wait_send()
            whole.wait_recv()

        @pl.when(s == k)
        def _():
            pltpu.make_async_copy(kept.at[s], kept.at[s], out_local.at[0]).wait()


def per_device_swept(start_amps, energies, thresholds, intersection):
    sectors = lax.axis_size("sec")
    groups = lax.axis_size("ch")
    energy_count, row_count, width_cols = start_amps.shape
    channel_count = intersection.shape[2]
    width = width_cols // 2 // sectors
    pairs = sectors // 2
    padded = jnp.concatenate([energies, jnp.broadcast_to(energies[:1], (-energy_count % 8,))])
    levels = jnp.broadcast_to(padded[:, None], (padded.shape[0], 128))
    aux = jnp.pad(thresholds, ((0, AUX_ROWS - 1), (0, channel_count - row_count)))
    own_block = jnp.concatenate([intersection[0], aux], axis=0)
    dma = pltpu.SemaphoreType.DMA
    stored = jax.ShapeDtypeStruct(start_amps.shape, jnp.bfloat16)
    swept = pl.pallas_call(
        functools.partial(sweep_kernel, sectors, groups),
        out_shape=stored,
        in_specs=[
            pl.BlockSpec(memory_space=pl.ANY),
            pl.BlockSpec(memory_space=pltpu.VMEM),
            pl.BlockSpec(memory_space=pl.ANY),
        ],
        out_specs=pl.BlockSpec(memory_space=pl.ANY),
        scratch_shapes=[
            pltpu.VMEM((sectors, groups, row_count + AUX_ROWS, channel_count), jnp.bfloat16),
            pltpu.VMEM((2, energy_count, channel_count, 2 * width), jnp.bfloat16),
            pltpu.VMEM((energy_count, channel_count, 2 * width), jnp.bfloat16),
            pltpu.VMEM((sectors, 2, energy_count, row_count, width), jnp.bfloat16),
            pltpu.VMEM((row_count, 128), jnp.float32),
            dma((3,)),
            dma((sectors, groups)),
            dma((pairs,)),
            dma((pairs, groups)),
            dma((pairs, groups)),
            dma((pairs, groups)),
            dma((energy_count, groups)),
            dma((groups,)),
            dma((groups,)),
            dma((sectors,)),
            dma((sectors,)),
            dma((1,)),
        ],
        compiler_params=pltpu.CompilerParams(
            collective_id=0, has_side_effects=True, vmem_limit_bytes=60 * 2**20
        ),
    )(start_amps, levels, own_block)
    return swept[None]


GATHERED_LIMIT = 24 * 2**20


def per_device(start_amps, energies, thresholds, intersection):
    sectors = lax.axis_size("sec")
    row_count, channel_count = intersection.shape[1:]
    gathered_bytes = sectors * channel_count**2 * intersection.dtype.itemsize
    even = sectors % 2 == 0 and (start_amps.shape[2] // 2) % (sectors * 128) == 0
    even = even and row_count % 128 == 0 and energies.shape[0] <= 40
    if even and gathered_bytes <= GATHERED_LIMIT:
        return per_device_swept(start_amps, energies, thresholds, intersection)
    return per_device_pipelined(start_amps, energies, thresholds, intersection)


def solution(mesh):
    in_specs = (P(None, "ch", None), P(), P("sec", "ch"), P("sec", "ch", None))
    out_specs = P("sec", None, "ch", None)
    return jax.shard_map(
        per_device, mesh=mesh, in_specs=in_specs, out_specs=out_specs, check_vma=False
    )
```
